1024 devices in a mesh: qa: 32 (over x, z_hi), qb: 32 (over y, z_lo, core).
Axes of the slice: x: 8, y: 8, z: 8 (z_hi: 4, z_lo: 2; z = z_hi * 2 + z_lo), core: 2. Of those that a mesh axis runs over, the one named last changes fastest.
Arguments:
- state: float32 [32, 32, 128, 8, 128], P('qa', 'qb'), may hold values from -6 to 6
- costate: float32 [32, 32, 128, 8, 128], P('qa', 'qb'), may hold values from -6 to 6
- gates: float32 [2, 4, 128, 128], replicated, may hold values from -0.5 to 0.5
- targets: int32 [2, 4], replicated, may hold values from 0 to 1
Outputs:
- start_state: float32 [32, 32, 128, 8, 128], P('qa', 'qb')
- start_costate: float32 [32, 32, 128, 8, 128], P('qa', 'qb')
- gate_grads: float32 [2, 4, 128, 128], replicated
The draws below stay inside these ranges and needn't reach their ends.
Inputs may be any that keep to these rules, and one draw needn't show every extreme that they name: `targets`: 0 means the gate acts on the last index, 1 on the third from last.
All inputs are finite; a program needn't handle non-finite values.
Results may differ from the reference program's by a relative error of at most 0.0003.
Values sent between devices are 32-bit elements; how exact they have to be, the bound alone decides.
A program may use at most 64 MiB of HBM per device.

```python
import jax
import jax.numpy as jnp
from jax import lax

GATE = 128
SLAB = 8
REST = 1048576
N_QA = 32
N_QB = 32


def touch_ends(result, rng, least, largest):
    longest = result.shape.index(max(result.shape))
    spots = []
    for shift in (0, 1):
        where = [jax.random.randint(jax.random.fold_in(rng, axis), (), 0, length) for axis, length in enumerate(result.shape)]
        where[longest] = (where[longest] + shift) % result.shape[longest]
        spots.append(tuple(where))
    return result.at[spots[0]].set(least).at[spots[1]].set(largest)


def levels(key, dims, pieces, least, largest):
    loudness, own = 1.0, jax.random.fold_in(key, 6)
    for dim, parts in pieces:
        steps = jnp.exp(jax.random.uniform(jax.random.fold_in(own, dim), (parts,), jnp.float32, least / len(pieces), largest / len(pieces)))
        loudness = loudness * jnp.repeat(steps, dims[dim] // parts).reshape([-1 if axis == dim else 1 for axis in range(len(dims))])
    return loudness


def gaussian(rng, extent, deviation, most, cuts=(), kind=jnp.bfloat16):
    gain = levels(rng, extent, cuts, -0.22, 0.18) if cuts else 1.0
    values = jax.random.normal(rng, extent, jnp.float32) * deviation * gain
    return jnp.minimum(jnp.maximum(values, -most), most).astype(kind)


def setup_inputs(seed: int = 0) -> dict:
    key_list = jax.random.split(jax.random.key(seed), 5)
    return {
        "state": gaussian(key_list[0], (N_QA, N_QB, GATE, SLAB, GATE), 1.0, 6.0, ((0, 32), (1, 32)), jnp.float32),
        "costate": gaussian(key_list[1], (N_QA, N_QB, GATE, SLAB, GATE), 1.0, 6.0, ((0, 32), (1, 32)), jnp.float32),
        "gates": gaussian(key_list[2], (2, 4, GATE, GATE), GATE ** -0.5, 0.5, (), jnp.float32),
        "targets": touch_ends(jax.random.randint(key_list[3], (2, 4), 0, 2), jax.random.fold_in(key_list[3], 1), 0, 1).astype(jnp.int32),
    }


def unapply(values, matrix, target):
    def apply_low(inner):
        return jnp.einsum('abmsi,ij->abmsj', inner, matrix, precision=lax.Precision.HIGHEST)

    def apply_middle(inner):
        return jnp.einsum('abisl,ij->abjsl', inner, matrix, precision=lax.Precision.HIGHEST)

    return lax.cond(target == 0, apply_low, apply_middle, values)


def gradient(adjoint, earlier, target):
    def from_low(inner):
        return jnp.einsum('abmsi,abmsj->ij', inner[0], inner[1], precision=lax.Precision.HIGHEST)

    def from_middle(inner):
        return jnp.einsum('abisl,abjsl->ij', inner[0], inner[1], precision=lax.Precision.HIGHEST)

    return lax.cond(target == 0, from_low, from_middle, (adjoint, earlier))


def swap_qubits(values, position, count):
    layout = values.shape
    remain = layout[2] // count
    split_view = values.reshape(layout[0], layout[1], count, remain, layout[3], layout[4])
    return jnp.swapaxes(split_view, position, 2).reshape(layout)


def reference(state, costate, gates, targets):
    amplitudes = state
    adjoint = costate
    results = [None, None]
    for block_index in (1, 0):
        grad_list = []
        for gate_index in (3, 2, 1, 0):
            matrix = gates[block_index, gate_index]
            target = targets[block_index, gate_index]
            earlier = unapply(amplitudes, matrix, target)
            grad_list.append(gradient(adjoint, earlier, target))
            adjoint = unapply(adjoint, matrix, target)
            amplitudes = earlier
        results[block_index] = jnp.stack(grad_list[::-1])
        if block_index == 1:
            amplitudes = swap_qubits(amplitudes, 1, N_QB)
            adjoint = swap_qubits(adjoint, 1, N_QB)
        else:
            amplitudes = swap_qubits(amplitudes, 0, N_QA)
            adjoint = swap_qubits(adjoint, 0, N_QA)
    gate_grads = jnp.stack(results) * (REST ** -0.5)
    return amplitudes, adjoint, gate_grads
```

```python
import functools

import jax
import jax.numpy as jnp
from jax import lax
from jax.experimental import pallas as pl
from jax.experimental.pallas import tpu as pltpu
from jax.sharding import PartitionSpec as P

F32 = jnp.float32
BF16 = jnp.bfloat16
HIGHEST = lax.Precision.HIGHEST
MESH = pl.DeviceIdType.MESH

CORES = 2
Z_HI = 4
CHUNK = 2


def split(value):
    high = value.astype(BF16)
    return high, (value - high.astype(F32)).astype(BF16)


def mul(left, right):
    return jnp.dot(left, right, preferred_element_type=F32)


def exact(left, right, left_dim=1, right_dim=0):
    return lax.dot_general(
        left, right, (((left_dim,), (right_dim,)), ((), ())), precision=HIGHEST, preferred_element_type=F32
    )


def main_kernel(
    cfg,
    targets,
    state,
    costate,
    gates,
    fin,
    total,
    send_b,
    recv_b,
    send_a,
    p_low,
    p_mid,
    q_pair,
    c_old,
    c_new,
    c_other,
    f_dup,
    f_low,
    f_adj,
    grads,
    raw,
    half_in,
    half,
    row_in,
    x_in,
    z_in,
    swap_send,
    swap_recv,
    own_sem,
    red_send,
    red_recv,
):
    NA, NB, ZH, C, SC, G, S, scale = cfg
    NC = S // SC
    X, J = NA // ZH, NB // C
    RB, RA = G // NB * SC, G // NA * SC
    a, b = lax.axis_index("qa"), lax.axis_index("qb")
    x, zh = a // ZH, a % ZH
    j, core = b // C, b % C

    barrier = pltpu.get_barrier_semaphore()

    def greet_b(k, carry):
        pl.semaphore_signal(barrier, inc=1, device_id=(a, (b + k) % NB), device_id_type=MESH)
        return carry

    def greet_a(k, carry):
        pl.semaphore_signal(barrier, inc=1, device_id=((a + k) % NA, b), device_id_type=MESH)
        return carry

    lax.fori_loop(1, NB, greet_b, 0)
    lax.fori_loop(1, NA, greet_a, 0)

    def products(block):
        eye_r = lax.broadcasted_iota(jnp.int32, (G, G), 0)
        eye_c = lax.broadcasted_iota(jnp.int32, (G, G), 1)
        prods = [(eye_r == eye_c).astype(F32)] * 2
        for step, g in enumerate((3, 2, 1, 0)):
            low = jnp.full((G, G), targets[block, g], jnp.int32) == 0
            mine = jnp.where(low, prods[0], prods[1])
            other = jnp.where(low, prods[1], prods[0])
            gate = gates[block * 4 + g]
            new = gate if step == 0 else exact(mine, gate)
            c_old[block, g] = mine
            c_new[block, g] = new * scale
            c_other[block, g] = other
            prods = [jnp.where(low, new, prods[0]), jnp.where(low, prods[1], new)]
        high, low_ = split(prods[0])
        p_low[block, :G, :G] = high
        p_low[block, :G, G:] = low_
        p_low[block, G:, :G] = high
        p_low[block, G:, G:] = jnp.zeros((G, G), BF16)
        high, low_ = split(prods[1].T)
        p_mid[block, :, :G] = high
        p_mid[block, :, G:] = low_

    def metrics(block):
        for g in range(4):
            other = c_other[block, g]
            high, low_ = split(exact(other, other, 1, 1))
            q_pair[block, g, :, :G] = high
            q_pair[block, g, :, G:] = low_

    def load_first(c, arr, s):
        ref = costate if arr else state
        return ref[pl.ds(c * SC + s, G, stride=S), :]

    def load_second(c, arr, s):
        return recv_b[c, arr, pl.ds(s, G, stride=SC), :]

    def transform(block, c, load, out):
        rows = jnp.concatenate([load(c, arr, s) for arr in range(2) for s in range(SC)], axis=0)
        high, low_ = split(rows)
        both = mul(jnp.concatenate([high, low_], axis=1), p_low[block])
        mid = both[:, :G] + both[:, G:]
        for arr in range(2):
            wide = jnp.concatenate([mid[(arr * SC + s) * G : (arr * SC + s + 1) * G] for s in range(SC)], axis=1)
            high, low_ = split(wide)
            done = mul(p_mid[block], jnp.concatenate([high, high], axis=0)) + mul(p_mid[block, :, :G], low_)
            for s in range(SC):
                out[c, arr, pl.ds(s, G, stride=SC), :] = done[:, s * G : (s + 1) * G]

    def derive(block, c, load):
        amps = [load(c, 0, s) for s in range(SC)]
        adjs = [load(c, 1, s) for s in range(SC)]
        for t in range(2):
            high, low_ = split(jnp.concatenate([v.T if t else v for v in amps], axis=1))
            f_dup[t, :G] = high
            f_dup[t, G:] = high
            f_low[t] = low_
            high, low_ = split(jnp.concatenate([v if t else v.T for v in adjs], axis=1))
            f_adj[t, :G] = high
            f_adj[t, G:] = low_
        for g in range(4):
            t = targets[block, g]
            wide = mul(q_pair[block, g], f_dup[t]) + mul(q_pair[block, g, :, :G], f_low[t])
            tall = jnp.concatenate([wide[:, s * G : (s + 1) * G] for s in range(SC)], axis=0)
            high, low_ = split(tall)
            quad = mul(f_adj[t], jnp.concatenate([high, low_], axis=1))
            grads[block, g] = grads[block, g] + (quad[:G, :G] + (quad[:G, G:] + quad[G:, :G]))

    def finish(block):
        per = raw.shape[2]
        for g in range(4):
            value = exact(c_old[block, g].T, exact(grads[block, g], c_new[block, g]))
            if G >= per:
                count = G // per
                raw[block, g * count : (g + 1) * count] = value.reshape(count, per, G)

    def spread(i, count):
        odd = i % 2
        return odd * ((i + 1) // 2) + (1 - odd) * (count - i // 2)

    def send_swap(c, which):
        src, dst, rows, n = (send_b, recv_b, RB, NB) if which == 0 else (send_a, fin, RA, NA)
        me = b if which == 0 else a
        mine = pl.ds(pl.multiple_of(me * rows, rows), rows)

        def one(i, carry):
            peer = (me + spread(i, n)) % n
            where = (a, peer) if which == 0 else (peer, b)
            pltpu.make_async_remote_copy(
                src_ref=src.at[c, :, pl.ds(pl.multiple_of(peer * rows, rows), rows), :],
                dst_ref=dst.at[c, :, mine, :],
                send_sem=swap_send.at[which, c],
                recv_sem=swap_recv.at[which, c],
                device_id=where,
                device_id_type=MESH,
            ).start()
            return carry

        lax.fori_loop(1, n, one, 0)
        pltpu.make_async_copy(src.at[c, :, mine, :], dst.at[c, :, mine, :], own_sem.at[which, c]).start()

    def wait_swap(c, which, sends):
        src, dst, rows, n = (send_b, recv_b, RB, NB) if which == 0 else (send_a, fin, RA, NA)
        me = b if which == 0 else a
        most = pl.ds(0, (n - 1) * rows)
        if sends:
            part = src.at[c, :, most, :]
            pltpu.make_async_copy(part, part, swap_send.at[which, c]).wait()
        else:
            part = dst.at[c, :, most, :]
            pltpu.make_async_copy(part, part, swap_recv.at[which, c]).wait()
            mine = pl.ds(pl.multiple_of(me * rows, rows), rows)
            pltpu.make_async_copy(src.at[c, :, mine, :], dst.at[c, :, mine, :], own_sem.at[which, c]).wait()

    def remote(src, dst, block, phase, where):
        return pltpu.make_async_remote_copy(
            src_ref=src,
            dst_ref=dst,
            send_sem=red_send.at[block, phase],
            recv_sem=red_recv.at[block, phase],
            device_id=where,
            device_id_type=MESH,
        )

    def took(ref, sems, block, phase):
        pltpu.make_async_copy(ref, ref, sems.at[block, phase]).wait()

    partner = (a, j * C + (1 - core))

    def reduce_core(block):
        remote(raw.at[block, pl.ds((1 - core) * J, J)], half_in.at[block], block, 0, partner).start()

    def reduce_rows(block):
        took(half_in.at[block], red_recv, block, 0)
        half[block] = raw[block, pl.ds(core * J, J)] + half_in[block]

        def one(k, carry):
            to = (j + k) % J
            remote(half.at[block, to], row_in.at[block, j], block, 1, (a, to * C + core)).start()
            return carry

        lax.fori_loop(1, J, one, 0)
        row_in[block, j] = half[block, j]

    def summed(ref, block, count):
        value = ref[block, 0]
        for i in range(1, count):
            value = value + ref[block, i]
        return value

    def reduce_x(block):
        took(row_in.at[block, pl.ds(0, J - 1)], red_recv, block, 1)
        x_in[block, x] = summed(row_in, block, J)

        def one(k, carry):
            remote(x_in.at[block, x], x_in.at[block, x], block, 2, ((x + k) % X * ZH + zh, b)).start()
            return carry

        lax.fori_loop(1, X, one, 0)

    def reduce_z(block):
        took(x_in.at[block, pl.ds(0, X - 1)], red_recv, block, 2)
        z_in[block, zh] = summed(x_in, block, X)

        def one(k, carry):
            remote(z_in.at[block, zh], z_in.at[block, zh], block, 3, (x * ZH + (zh + k) % ZH, b)).start()
            return carry

        lax.fori_loop(1, ZH, one, 0)

    def gather_rows(block):
        took(z_in.at[block, pl.ds(0, ZH - 1)], red_recv, block, 3)
        slot = core * J + j
        total[block, slot] = summed(z_in, block, ZH)

        def one(k, carry):
            to = (j + k) % J
            remote(total.at[block, slot], total.at[block, slot], block, 4, (a, to * C + core)).start()
            return carry

        lax.fori_loop(1, J, one, 0)

    def gather_core(block):
        took(total.at[block, pl.ds(0, J - 1)], red_recv, block, 4)
        part = total.at[block, pl.ds(core * J, J)]
        remote(part, part, block, 5, partner).start()

    def gather_done(block):
        took(half_in.at[block], red_recv, block, 5)

    grads[...] = jnp.zeros_like(grads)
    products(1)
    pl.semaphore_wait(barrier, NA + NB - 2)

    def first(c, carry):
        transform(1, c, load_first, send_b)
        send_swap(c, 0)
        return carry

    lax.fori_loop(0, NC, first, 0)
    metrics(1)

    def first_derive(c, carry):
        derive(1, c, load_first)
        return carry

    lax.fori_loop(0, NC, first_derive, 0)
    finish(1)
    reduce_core(1)
    products(0)
    metrics(0)
    reduce_rows(1)

    def second(c, carry):
        wait_swap(c, 0, False)
        transform(0, c, load_second, send_a)
        send_swap(c, 1)
        derive(0, c, load_second)
        return carry

    lax.fori_loop(0, NC, second, 0)
    finish(0)
    reduce_core(0)
    reduce_x(1)
    reduce_rows(0)
    reduce_z(1)
    reduce_x(0)
    gather_rows(1)
    reduce_z(0)
    gather_core(1)
    gather_rows(0)
    gather_done(1)
    gather_core(0)
    gather_done(0)

    def ending(c, carry):
        wait_swap(c, 1, False)
        wait_swap(c, 0, True)
        wait_swap(c, 1, True)
        return carry

    lax.fori_loop(0, NC, ending, 0)
    for block in range(2):
        took(half_in.at[block], red_send, block, 0)
        took(row_in.at[block, pl.ds(0, J - 1)], red_send, block, 1)
        took(x_in.at[block, pl.ds(0, X - 1)], red_send, block, 2)
        took(z_in.at[block, pl.ds(0, ZH - 1)], red_send, block, 3)
        took(total.at[block, pl.ds(0, J - 1)], red_send, block, 4)
        took(half_in.at[block], red_send, block, 5)


def layout_kernel(cfg, fin, total, out_state, out_costate, out_grads):
    NA, NB, ZH, C, SC, G, S, scale = cfg
    for arr, out in ((0, out_state), (1, out_costate)):
        for c in range(S // SC):
            for s in range(SC):
                out[pl.ds(c * SC + s, G, stride=S), :] = fin[c, arr, pl.ds(s, G, stride=SC), :]
    out_grads[...] = total[...]


def shards(zh, cores, state, costate, gates, targets):
    NA, NB = lax.axis_size("qa"), lax.axis_size("qb")
    layout = state.shape
    G, S, L = layout[2:]
    SC = CHUNK
    NC = S // SC
    X, J = NA // zh, NB // cores
    scale = float(NA * NB * G * S) ** -0.5
    cfg = (NA, NB, zh, cores, SC, G, S, scale)
    per = 4 * G // NB
    vmem = pl.BlockSpec(memory_space=pltpu.VMEM)
    fin, total = pl.pallas_call(
        functools.partial(main_kernel, cfg),
        out_shape=(
            jax.ShapeDtypeStruct((NC, 2, G * SC, L), F32),
            jax.ShapeDtypeStruct((2, NB, per, L), F32),
        ),
        in_specs=[pl.BlockSpec(memory_space=pltpu.SMEM), vmem, vmem, vmem],
        out_specs=(vmem, vmem),
        scratch_shapes=[
            pltpu.VMEM((NC, 2, G * SC, L), F32),
            pltpu.VMEM((NC, 2, G * SC, L), F32),
            pltpu.VMEM((NC, 2, G * SC, L), F32),
            pltpu.VMEM((2, 2 * G, 2 * G), BF16),
            pltpu.VMEM((2, G, 2 * G), BF16),
            pltpu.VMEM((2, 4, G, 2 * G), BF16),
            pltpu.VMEM((2, 4, G, G), F32),
            pltpu.VMEM((2, 4, G, G), F32),
            pltpu.VMEM((2, 4, G, G), F32),
            pltpu.VMEM((2, 2 * G, SC * G), BF16),
            pltpu.VMEM((2, G, SC * G), BF16),
            pltpu.VMEM((2, 2 * G, SC * G), BF16),
            pltpu.VMEM((2, 4, G, G), F32),
            pltpu.VMEM((2, NB, per, L), F32),
            pltpu.VMEM((2, J, per, L), F32),
            pltpu.VMEM((2, J, per, L), F32),
            pltpu.VMEM((2, J, per, L), F32),
            pltpu.VMEM((2, X, per, L), F32),
            pltpu.VMEM((2, zh, per, L), F32),
            pltpu.SemaphoreType.DMA((2, NC)),
            pltpu.SemaphoreType.DMA((2, NC)),
            pltpu.SemaphoreType.DMA((2, NC)),
            pltpu.SemaphoreType.DMA((2, 6)),
            pltpu.SemaphoreType.DMA((2, 6)),
        ],
        compiler_params=pltpu.CompilerParams(collective_id=0, has_side_effects=True),
        name="adjoint_main",
    )(targets, state.reshape(G * S, L), costate.reshape(G * S, L), gates.reshape(8, G, G))
    out_state, out_costate, grads = pl.pallas_call(
        functools.partial(layout_kernel, cfg),
        out_shape=(
            jax.ShapeDtypeStruct((G * S, L), F32),
            jax.ShapeDtypeStruct((G * S, L), F32),
            jax.ShapeDtypeStruct((2, NB, per, L), F32),
        ),
        in_specs=[vmem, vmem],
        out_specs=(vmem, vmem, vmem),
        name="adjoint_layout",
    )(fin, total)
    return out_state.reshape(layout), out_costate.reshape(layout), grads.reshape(2, 4, G, G)


def build(mesh, zh, cores):
    in_specs = (P("qa", "qb", None, None, None), P("qa", "qb", None, None, None), P(), P())
    out_specs = (P("qa", "qb", None, None, None), P("qa", "qb", None, None, None), P())
    return jax.shard_map(
        functools.partial(shards, zh, cores), mesh=mesh, in_specs=in_specs, out_specs=out_specs, check_vma=False
    )


def solution(mesh):
    return build(mesh, Z_HI, CORES)
```

```python
import functools

import jax
import jax.numpy as jnp
from jax import lax
from jax.experimental import pallas as pl
from jax.experimental.pallas import tpu as pltpu
from jax.sharding import PartitionSpec as P

F32 = jnp.float32
BF16 = jnp.bfloat16
HIGHEST = lax.Precision.HIGHEST
MESH = pl.DeviceIdType.MESH

CORES = 2
Z_HI = 4
CHUNK = 2


def split(value):
    high = value.astype(BF16)
    return high, (value - high.astype(F32)).astype(BF16)


def mul(left, right):
    return jnp.dot(left, right, preferred_element_type=F32)


def exact(left, right, left_dim=1, right_dim=0):
    return lax.dot_general(
        left, right, (((left_dim,), (right_dim,)), ((), ())), precision=HIGHEST, preferred_element_type=F32
    )


def main_kernel(
    cfg,
    targets,
    state,
    costate,
    gates,
    fin,
    total_lo,
    total,
    send_b,
    recv_b,
    send_a,
    p_low,
    p_mid,
    q_pair,
    o_pair,
    n_dup,
    n_low,
    c_other,
    f_dup,
    f_low,
    f_adj,
    grads,
    raw,
    raw_lo,
    half_in,
    half,
    row_in,
    x_in,
    z_in,
    part_in,
    share_in,
    swap_send,
    swap_recv,
    own_sem,
    red_send,
    red_recv,
    low_send,
    low_recv,
):
    NA, NB, ZH, C, SC, G, S, scale = cfg
    NC = S // SC
    X, J = NA // ZH, NB // C
    RB, RA = G // NB * SC, G // NA * SC
    a, b = lax.axis_index("qa"), lax.axis_index("qb")
    x, zh = a // ZH, a % ZH
    j, core = b // C, b % C

    barrier = pltpu.get_barrier_semaphore()

    def greet_b(k, carry):
        pl.semaphore_signal(barrier, inc=1, device_id=(a, (b + k) % NB), device_id_type=MESH)
        return carry

    def greet_a(k, carry):
        pl.semaphore_signal(barrier, inc=1, device_id=((a + k) % NA, b), device_id_type=MESH)
        return carry

    lax.fori_loop(1, NB, greet_b, 0)
    lax.fori_loop(1, NA, greet_a, 0)

    def products(block):
        eye_r = lax.broadcasted_iota(jnp.int32, (G, G), 0)
        eye_c = lax.broadcasted_iota(jnp.int32, (G, G), 1)
        prods = [(eye_r == eye_c).astype(F32)] * 2
        for step, g in enumerate((3, 2, 1, 0)):
            low = jnp.full((G, G), targets[block, g], jnp.int32) == 0
            mine = jnp.where(low, prods[0], prods[1])
            other = jnp.where(low, prods[1], prods[0])
            gate = gates[block * 4 + g]
            new = gate if step == 0 else exact(mine, gate)
            high, low_ = split(mine.T)
            o_pair[block, g, :, :G] = high
            o_pair[block, g, :, G:] = low_
            high, low_ = split(new * scale)
            n_dup[block, g, :G] = high
            n_dup[block, g, G:] = high
            n_low[block, g] = low_
            c_other[block, g] = other
            prods = [jnp.where(low, new, prods[0]), jnp.where(low, prods[1], new)]
        high, low_ = split(prods[0])
        p_low[block, :G, :G] = high
        p_low[block, :G, G:] = low_
        p_low[block, G:, :G] = high
        p_low[block, G:, G:] = jnp.zeros((G, G), BF16)
        high, low_ = split(prods[1].T)
        p_mid[block, :, :G] = high
        p_mid[block, :, G:] = low_

    def metrics(block):
        for g in range(4):
            other = c_other[block, g]
            high, low_ = split(exact(other, other, 1, 1))
            q_pair[block, g, :, :G] = high
            q_pair[block, g, :, G:] = low_

    def load_first(c, arr, s):
        ref = costate if arr else state
        return ref[pl.ds(c * SC + s, G, stride=S), :]

    def load_second(c, arr, s):
        return recv_b[c, arr, pl.ds(s, G, stride=SC), :]

    def transform(block, c, load, out):
        rows = jnp.concatenate([load(c, arr, s) for arr in range(2) for s in range(SC)], axis=0)
        high, low_ = split(rows)
        both = mul(jnp.concatenate([high, low_], axis=1), p_low[block])
        mid = both[:, :G] + both[:, G:]
        for arr in range(2):
            wide = jnp.concatenate([mid[(arr * SC + s) * G : (arr * SC + s + 1) * G] for s in range(SC)], axis=1)
            high, low_ = split(wide)
            done = mul(p_mid[block], jnp.concatenate([high, high], axis=0)) + mul(p_mid[block, :, :G], low_)
            for s in range(SC):
                out[c, arr, pl.ds(s, G, stride=SC), :] = done[:, s * G : (s + 1) * G]

    def prepare(c, load):
        amps = [load(c, 0, s) for s in range(SC)]
        adjs = [load(c, 1, s) for s in range(SC)]
        for t in range(2):
            high, low_ = split(jnp.concatenate([v.T if t else v for v in amps], axis=1))
            f_dup[t, :G] = high
            f_dup[t, G:] = high
            f_low[t] = low_
            high, low_ = split(jnp.concatenate([v if t else v.T for v in adjs], axis=1))
            f_adj[t, :G] = high
            f_adj[t, G:] = low_

    def derive(block, chosen):
        for g in chosen:
            t = targets[block, g]
            wide = mul(q_pair[block, g], f_dup[t]) + mul(q_pair[block, g, :, :G], f_low[t])
            tall = jnp.concatenate([wide[:, s * G : (s + 1) * G] for s in range(SC)], axis=0)
            high, low_ = split(tall)
            quad = mul(f_adj[t], jnp.concatenate([high, low_], axis=1))
            grads[block, g] = grads[block, g] + (quad[:G, :G] + (quad[:G, G:] + quad[G:, :G]))

    def finished(block, g):
        high, low_ = split(grads[block, g])
        part = mul(jnp.concatenate([high, low_], axis=1), n_dup[block, g]) + mul(high, n_low[block, g])
        high, low_ = split(part)
        return mul(o_pair[block, g], jnp.concatenate([high, high], axis=0)) + mul(o_pair[block, g, :, :G], low_)

    def spread(i, count):
        odd = i % 2
        return odd * ((i + 1) // 2) + (1 - odd) * (count - i // 2)

    def send_swap(c, which):
        src, dst, rows, n = (send_b, recv_b, RB, NB) if which == 0 else (send_a, fin, RA, NA)
        me = b if which == 0 else a
        mine = pl.ds(pl.multiple_of(me * rows, rows), rows)

        def one(i, carry):
            peer = (me + spread(i, n)) % n
            where = (a, peer) if which == 0 else (peer, b)
            pltpu.make_async_remote_copy(
                src_ref=src.at[c, :, pl.ds(pl.multiple_of(peer * rows, rows), rows), :],
                dst_ref=dst.at[c, :, mine, :],
                send_sem=swap_send.at[which, c],
                recv_sem=swap_recv.at[which, c],
                device_id=where,
                device_id_type=MESH,
            ).start()
            return carry

        lax.fori_loop(1, n, one, 0)
        pltpu.make_async_copy(src.at[c, :, mine, :], dst.at[c, :, mine, :], own_sem.at[which, c]).start()

    def wait_swap(c, which, sends):
        src, dst, rows, n = (send_b, recv_b, RB, NB) if which == 0 else (send_a, fin, RA, NA)
        me = b if which == 0 else a
        most = pl.ds(0, (n - 1) * rows)
        if sends:
            part = src.at[c, :, most, :]
            pltpu.make_async_copy(part, part, swap_send.at[which, c]).wait()
        else:
            part = dst.at[c, :, most, :]
            pltpu.make_async_copy(part, part, swap_recv.at[which, c]).wait()
            mine = pl.ds(pl.multiple_of(me * rows, rows), rows)
            pltpu.make_async_copy(src.at[c, :, mine, :], dst.at[c, :, mine, :], own_sem.at[which, c]).wait()

    def remote(src, dst, send_sem, recv_sem, where):
        return pltpu.make_async_remote_copy(
            src_ref=src, dst_ref=dst, send_sem=send_sem, recv_sem=recv_sem, device_id=where, device_id_type=MESH
        )

    def took(ref, sem):
        pltpu.make_async_copy(ref, ref, sem).wait()

    def summed(ref, count):
        value = ref[0]
        for i in range(1, count):
            value = value + ref[i]
        return value

    partner = (a, j * C + (1 - core))

    def reduce_core():
        remote(raw.at[pl.ds((1 - core) * J, J)], half_in, red_send.at[0], red_recv.at[0], partner).start()

    def reduce_rows():
        took(half_in, red_recv.at[0])
        half[...] = raw[pl.ds(core * J, J)] + half_in[...]

        def one(k, carry):
            to = (j + k) % J
            remote(half.at[to], row_in.at[j], red_send.at[1], red_recv.at[1], (a, to * C + core)).start()
            return carry

        lax.fori_loop(1, J, one, 0)
        row_in[j] = half[j]

    def reduce_x():
        took(row_in.at[pl.ds(0, J - 1)], red_recv.at[1])
        x_in[x] = summed(row_in, J)

        def one(k, carry):
            to = ((x + k) % X * ZH + zh, b)
            remote(x_in.at[x], x_in.at[x], red_send.at[2], red_recv.at[2], to).start()
            return carry

        lax.fori_loop(1, X, one, 0)

    def reduce_z():
        took(x_in.at[pl.ds(0, X - 1)], red_recv.at[2])
        z_in[zh] = summed(x_in, X)

        def one(k, carry):
            to = (x * ZH + (zh + k) % ZH, b)
            remote(z_in.at[zh], z_in.at[zh], red_send.at[3], red_recv.at[3], to).start()
            return carry

        lax.fori_loop(1, ZH, one, 0)

    def gather_rows():
        took(z_in.at[pl.ds(0, ZH - 1)], red_recv.at[3])
        slot = core * J + j
        total[slot] = summed(z_in, ZH)

        def one(k, carry):
            to = (j + k) % J
            remote(total.at[slot], total.at[slot], red_send.at[4], red_recv.at[4], (a, to * C + core)).start()
            return carry

        lax.fori_loop(1, J, one, 0)

    def gather_core():
        took(total.at[pl.ds(0, J - 1)], red_recv.at[4])
        part = total.at[pl.ds(core * J, J)]
        remote(part, part, red_send.at[5], red_recv.at[5], partner).start()

    def gather_done():
        took(half_in, red_recv.at[5])

    def low_scatter(q):
        def one(i, carry):
            to = (b + spread(i, NB)) % NB
            remote(raw_lo.at[q, to], part_in.at[q, b], low_send.at[q, 0], low_recv.at[q, 0], (a, to)).start()
            return carry

        lax.fori_loop(1, NB, one, 0)
        part_in[q, b] = raw_lo[q, b]

    def low_share(q):
        took(part_in.at[q, pl.ds(0, NB - 1)], low_recv.at[q, 0])
        share_in[q, a] = summed(part_in.at[q], NB)

        def one(i, carry):
            to = ((a + spread(i, NA)) % NA, b)
            remote(share_in.at[q, a], share_in.at[q, a], low_send.at[q, 1], low_recv.at[q, 1], to).start()
            return carry

        lax.fori_loop(1, NA, one, 0)

    def low_gather(q):
        took(share_in.at[q, pl.ds(0, NA - 1)], low_recv.at[q, 1])
        total_lo[q, b] = summed(share_in.at[q], NA)

        def one(i, carry):
            to = (a, (b + spread(i, NB)) % NB)
            remote(total_lo.at[q, b], total_lo.at[q, b], low_send.at[q, 2], low_recv.at[q, 2], to).start()
            return carry

        lax.fori_loop(1, NB, one, 0)

    def low_done(q):
        took(total_lo.at[q, pl.ds(0, NB - 1)], low_recv.at[q, 2])

    grads[...] = jnp.zeros_like(grads)
    products(1)
    transform(1, 0, load_first, send_b)
    pl.semaphore_wait(barrier, NA + NB - 2)
    send_swap(0, 0)

    def first(c, carry):
        transform(1, c, load_first, send_b)
        send_swap(c, 0)
        return carry

    lax.fori_loop(1, NC, first, 0)
    metrics(1)

    def first_derive(c, carry):
        prepare(c, load_first)
        derive(1, range(4))
        return carry

    lax.fori_loop(0, NC, first_derive, 0)
    per = raw.shape[1]
    for g in range(4):
        raw[g * G // per : (g + 1) * G // per] = finished(1, g).reshape(G // per, per, G)
    reduce_core()
    products(0)
    metrics(0)
    reduce_rows()

    def second(c, carry):
        wait_swap(c, 0, False)
        transform(0, c, load_second, send_a)
        send_swap(c, 1)
        prepare(c, load_second)
        derive(0, range(4))
        return carry

    lax.fori_loop(0, NC - 1, second, 0)
    wait_swap(NC - 1, 0, False)
    prepare(NC - 1, load_second)
    per = raw_lo.shape[2]
    for q in range(2):
        derive(0, (2 * q, 2 * q + 1))
        for i in range(2):
            raw_lo[q, i * G // per : (i + 1) * G // per] = finished(0, 2 * q + i).reshape(G // per, per, G)
        low_scatter(q)
    reduce_x()
    transform(0, NC - 1, load_second, send_a)
    send_swap(NC - 1, 1)
    low_share(0)
    low_share(1)
    reduce_z()
    gather_rows()
    low_gather(0)
    low_gather(1)
    gather_core()
    gather_done()
    low_done(0)
    low_done(1)

    def ending(c, carry):
        wait_swap(c, 1, False)
        wait_swap(c, 0, True)
        wait_swap(c, 1, True)
        return carry

    lax.fori_loop(0, NC, ending, 0)
    took(half_in, red_send.at[0])
    took(row_in.at[pl.ds(0, J - 1)], red_send.at[1])
    took(x_in.at[pl.ds(0, X - 1)], red_send.at[2])
    took(z_in.at[pl.ds(0, ZH - 1)], red_send.at[3])
    took(total.at[pl.ds(0, J - 1)], red_send.at[4])
    took(half_in, red_send.at[5])
    for q in range(2):
        took(part_in.at[q, pl.ds(0, NB - 1)], low_send.at[q, 0])
        took(share_in.at[q, pl.ds(0, NA - 1)], low_send.at[q, 1])
        took(total_lo.at[q, pl.ds(0, NB - 1)], low_send.at[q, 2])


def layout_kernel(S, SC, fin, total_lo, total, out_state, out_costate, out_grads):
    rows = out_state.shape[0] // S
    for arr, out in ((0, out_state), (1, out_costate)):
        for c in range(S // SC):
            for s in range(SC):
                out[pl.ds(c * SC + s, rows, stride=S), :] = fin[c, arr, pl.ds(s, rows, stride=SC), :]
    out_grads[0] = total_lo[...]
    out_grads[1] = total[...]


def shards(zh, cores, state, costate, gates, targets):
    NA, NB = lax.axis_size("qa"), lax.axis_size("qb")
    layout = state.shape
    G, S, L = layout[2:]
    SC = CHUNK
    NC = S // SC
    X, J = NA // zh, NB // cores
    scale = float(NA * NB * G * S) ** -0.5
    cfg = (NA, NB, zh, cores, SC, G, S, scale)
    per, per_lo = 4 * G // NB, 2 * G // NB
    vmem = pl.BlockSpec(memory_space=pltpu.VMEM)
    fin, total_lo, total = pl.pallas_call(
        functools.partial(main_kernel, cfg),
        out_shape=(
            jax.ShapeDtypeStruct((NC, 2, G * SC, L), F32),
            jax.ShapeDtypeStruct((2, NB, per_lo, L), F32),
            jax.ShapeDtypeStruct((NB, per, L), F32),
        ),
        in_specs=[pl.BlockSpec(memory_space=pltpu.SMEM), vmem, vmem, vmem],
        out_specs=(vmem, vmem, vmem),
        scratch_shapes=[
            pltpu.VMEM((NC, 2, G * SC, L), F32),
            pltpu.VMEM((NC, 2, G * SC, L), F32),
            pltpu.VMEM((NC, 2, G * SC, L), F32),
            pltpu.VMEM((2, 2 * G, 2 * G), BF16),
            pltpu.VMEM((2, G, 2 * G), BF16),
            pltpu.VMEM((2, 4, G, 2 * G), BF16),
            pltpu.VMEM((2, 4, G, 2 * G), BF16),
            pltpu.VMEM((2, 4, 2 * G, G), BF16),
            pltpu.VMEM((2, 4, G, G), BF16),
            pltpu.VMEM((2, 4, G, G), F32),
            pltpu.VMEM((2, 2 * G, SC * G), BF16),
            pltpu.VMEM((2, G, SC * G), BF16),
            pltpu.VMEM((2, 2 * G, SC * G), BF16),
            pltpu.VMEM((2, 4, G, G), F32),
            pltpu.VMEM((NB, per, L), F32),
            pltpu.VMEM((2, NB, per_lo, L), F32),
            pltpu.VMEM((J, per, L), F32),
            pltpu.VMEM((J, per, L), F32),
            pltpu.VMEM((J, per, L), F32),
            pltpu.VMEM((X, per, L), F32),
            pltpu.VMEM((zh, per, L), F32),
            pltpu.VMEM((2, NB, per_lo, L), F32),
            pltpu.VMEM((2, NA, per_lo, L), F32),
            pltpu.SemaphoreType.DMA((2, NC)),
            pltpu.SemaphoreType.DMA((2, NC)),
            pltpu.SemaphoreType.DMA((2, NC)),
            pltpu.SemaphoreType.DMA((6,)),
            pltpu.SemaphoreType.DMA((6,)),
            pltpu.SemaphoreType.DMA((2, 3)),
            pltpu.SemaphoreType.DMA((2, 3)),
        ],
        compiler_params=pltpu.CompilerParams(collective_id=0, has_side_effects=True),
        name="adjoint_main",
    )(targets, state.reshape(G * S, L), costate.reshape(G * S, L), gates.reshape(8, G, G))
    steps = 4
    out_state, out_costate, grads = pl.pallas_call(
        functools.partial(layout_kernel, S, SC),
        grid=(steps,),
        out_shape=(
            jax.ShapeDtypeStruct((G * S, L), F32),
            jax.ShapeDtypeStruct((G * S, L), F32),
            jax.ShapeDtypeStruct((2, 4 * G, L), F32),
        ),
        in_specs=[
            pl.BlockSpec((NC, 2, G * SC // steps, L), lambda i: (0, 0, i, 0)),
            pl.BlockSpec((4 * G // steps, L), lambda i: (i, 0)),
            pl.BlockSpec((4 * G // steps, L), lambda i: (i, 0)),
        ],
        out_specs=(
            pl.BlockSpec((G * S // steps, L), lambda i: (i, 0)),
            pl.BlockSpec((G * S // steps, L), lambda i: (i, 0)),
            pl.BlockSpec((2, 4 * G // steps, L), lambda i: (0, i, 0)),
        ),
        name="adjoint_layout",
    )(fin, total_lo.reshape(4 * G, L), total.reshape(4 * G, L))
    return out_state.reshape(layout), out_costate.reshape(layout), grads.reshape(2, 4, G, G)


def build(mesh, zh, cores):
    in_specs = (P("qa", "qb", None, None, None), P("qa", "qb", None, None, None), P(), P())
    out_specs = (P("qa", "qb", None, None, None), P("qa", "qb", None, None, None), P())
    return jax.shard_map(
        functools.partial(shards, zh, cores), mesh=mesh, in_specs=in_specs, out_specs=out_specs, check_vma=False
    )


def solution(mesh):
    return build(mesh, Z_HI, CORES)
```

```python
import functools

import jax
import jax.numpy as jnp
from jax import lax
from jax.experimental import pallas as pl
from jax.experimental.pallas import tpu as pltpu
from jax.sharding import PartitionSpec as P

F32 = jnp.float32
BF16 = jnp.bfloat16
HIGHEST = lax.Precision.HIGHEST
MESH = pl.DeviceIdType.MESH

CORES = 2
Z_HI = 4
CHUNK = 2


def split(value):
    high = value.astype(BF16)
    return high, (value - high.astype(F32)).astype(BF16)


def mul(left, right):
    return jnp.dot(left, right, preferred_element_type=F32)


def exact(left, right, left_dim=1, right_dim=0):
    return lax.dot_general(
        left, right, (((left_dim,), (right_dim,)), ((), ())), precision=HIGHEST, preferred_element_type=F32
    )


def main_kernel(
    cfg,
    targets,
    state_in,
    costate_in,
    gates_in,
    fin,
    total,
    state,
    costate,
    gates,
    load_sem,
    send_b,
    recv_b,
    send_a,
    p_low,
    p_mid,
    q_pair,
    o_pair,
    n_dup,
    n_low,
    c_other,
    f_dup,
    f_low,
    f_adj,
    grads,
    raw,
    half_in,
    half,
    row_in,
    x_in,
    z_in,
    swap_send,
    swap_recv,
    own_sem,
    red_send,
    red_recv,
):
    NA, NB, ZH, C, SC, G, S, scale = cfg
    NC = S // SC
    X, J = NA // ZH, NB // C
    RB, RA = G // NB * SC, G // NA * SC
    a, b = lax.axis_index("qa"), lax.axis_index("qb")
    x, zh = a // ZH, a % ZH
    j, core = b // C, b % C

    barrier = pltpu.get_barrier_semaphore()

    def greet_b(k, carry):
        pl.semaphore_signal(barrier, inc=1, device_id=(a, (b + k) % NB), device_id_type=MESH)
        return carry

    def greet_a(k, carry):
        pl.semaphore_signal(barrier, inc=1, device_id=((a + k) % NA, b), device_id_type=MESH)
        return carry

    loads = [
        pltpu.make_async_copy(src, dst, load_sem.at[i])
        for i, (src, dst) in enumerate(((gates_in, gates), (state_in, state), (costate_in, costate)))
    ]
    for load in loads:
        load.start()
    lax.fori_loop(1, NB, greet_b, 0)
    lax.fori_loop(1, NA, greet_a, 0)

    def products(block):
        eye_r = lax.broadcasted_iota(jnp.int32, (G, G), 0)
        eye_c = lax.broadcasted_iota(jnp.int32, (G, G), 1)
        prods = [(eye_r == eye_c).astype(F32)] * 2
        for step, g in enumerate((3, 2, 1, 0)):
            low = jnp.full((G, G), targets[block, g], jnp.int32) == 0
            mine = jnp.where(low, prods[0], prods[1])
            other = jnp.where(low, prods[1], prods[0])
            gate = gates[block * 4 + g]
            new = gate if step == 0 else exact(mine, gate)
            high, low_ = split(mine.T)
            o_pair[block, g, :, :G] = high
            o_pair[block, g, :, G:] = low_
            high, low_ = split(new * scale)
            n_dup[block, g, :G] = high
            n_dup[block, g, G:] = high
            n_low[block, g] = low_
            c_other[block, g] = other
            prods = [jnp.where(low, new, prods[0]), jnp.where(low, prods[1], new)]
        high, low_ = split(prods[0])
        p_low[block, :G, :G] = high
        p_low[block, :G, G:] = low_
        p_low[block, G:, :G] = high
        p_low[block, G:, G:] = jnp.zeros((G, G), BF16)
        high, low_ = split(prods[1].T)
        p_mid[block, :, :G] = high
        p_mid[block, :, G:] = low_

    def metrics(block):
        for g in range(4):
            other = c_other[block, g]
            high, low_ = split(exact(other, other, 1, 1))
            q_pair[block, g, :, :G] = high
            q_pair[block, g, :, G:] = low_

    def load_first(c, arr, s):
        ref = costate if arr else state
        return ref[pl.ds(c * SC + s, G, stride=S), :]

    def load_second(c, arr, s):
        return recv_b[c, arr, pl.ds(s, G, stride=SC), :]

    def transform(block, c, load, out):
        rows = jnp.concatenate([load(c, arr, s) for arr in range(2) for s in range(SC)], axis=0)
        high, low_ = split(rows)
        both = mul(jnp.concatenate([high, low_], axis=1), p_low[block])
        mid = both[:, :G] + both[:, G:]
        for arr in range(2):
            wide = jnp.concatenate([mid[(arr * SC + s) * G : (arr * SC + s + 1) * G] for s in range(SC)], axis=1)
            high, low_ = split(wide)
            done = mul(p_mid[block], jnp.concatenate([high, high], axis=0)) + mul(p_mid[block, :, :G], low_)
            for s in range(SC):
                out[c, arr, pl.ds(s, G, stride=SC), :] = done[:, s * G : (s + 1) * G]

    def derive(block, c, load):
        amps = [load(c, 0, s) for s in range(SC)]
        adjs = [load(c, 1, s) for s in range(SC)]
        for t in range(2):
            high, low_ = split(jnp.concatenate([v.T if t else v for v in amps], axis=1))
            f_dup[t, :G] = high
            f_dup[t, G:] = high
            f_low[t] = low_
            high, low_ = split(jnp.concatenate([v if t else v.T for v in adjs], axis=1))
            f_adj[t, :G] = high
            f_adj[t, G:] = low_
        for g in range(4):
            t = targets[block, g]
            wide = mul(q_pair[block, g], f_dup[t]) + mul(q_pair[block, g, :, :G], f_low[t])
            tall = jnp.concatenate([wide[:, s * G : (s + 1) * G] for s in range(SC)], axis=0)
            high, low_ = split(tall)
            quad = mul(f_adj[t], jnp.concatenate([high, low_], axis=1))
            grads[block, g] = grads[block, g] + (quad[:G, :G] + (quad[:G, G:] + quad[G:, :G]))

    def finish(block):
        per = raw.shape[2]
        for g in range(4):
            high, low_ = split(grads[block, g])
            part = mul(jnp.concatenate([high, low_], axis=1), n_dup[block, g]) + mul(high, n_low[block, g])
            high, low_ = split(part)
            value = mul(o_pair[block, g], jnp.concatenate([high, high], axis=0)) + mul(o_pair[block, g, :, :G], low_)
            raw[block, g * G // per : (g + 1) * G // per] = value.reshape(G // per, per, G)

    def spread(i, count):
        odd = i % 2
        return odd * ((i + 1) // 2) + (1 - odd) * (count - i // 2)

    def send_swap(c, which):
        src, dst, rows, n = (send_b, recv_b, RB, NB) if which == 0 else (send_a, fin, RA, NA)
        me = b if which == 0 else a
        mine = pl.ds(pl.multiple_of(me * rows, rows), rows)

        def one(i, carry):
            peer = (me + spread(i, n)) % n
            where = (a, peer) if which == 0 else (peer, b)
            pltpu.make_async_remote_copy(
                src_ref=src.at[c, :, pl.ds(pl.multiple_of(peer * rows, rows), rows), :],
                dst_ref=dst.at[c, :, mine, :],
                send_sem=swap_send.at[which, c],
                recv_sem=swap_recv.at[which, c],
                device_id=where,
                device_id_type=MESH,
            ).start()
            return carry

        lax.fori_loop(1, n, one, 0)
        pltpu.make_async_copy(src.at[c, :, mine, :], dst.at[c, :, mine, :], own_sem.at[which, c]).start()

    def wait_swap(c, which, sends):
        src, dst, rows, n = (send_b, recv_b, RB, NB) if which == 0 else (send_a, fin, RA, NA)
        me = b if which == 0 else a
        most = pl.ds(0, (n - 1) * rows)
        if sends:
            part = src.at[c, :, most, :]
            pltpu.make_async_copy(part, part, swap_send.at[which, c]).wait()
        else:
            part = dst.at[c, :, most, :]
            pltpu.make_async_copy(part, part, swap_recv.at[which, c]).wait()
            mine = pl.ds(pl.multiple_of(me * rows, rows), rows)
            pltpu.make_async_copy(src.at[c, :, mine, :], dst.at[c, :, mine, :], own_sem.at[which, c]).wait()

    def remote(src, dst, block, phase, where):
        return pltpu.make_async_remote_copy(
            src_ref=src,
            dst_ref=dst,
            send_sem=red_send.at[block, phase],
            recv_sem=red_recv.at[block, phase],
            device_id=where,
            device_id_type=MESH,
        )

    def took(ref, sems, block, phase):
        pltpu.make_async_copy(ref, ref, sems.at[block, phase]).wait()

    partner = (a, j * C + (1 - core))

    def reduce_core(block):
        remote(raw.at[block, pl.ds((1 - core) * J, J)], half_in.at[block], block, 0, partner).start()

    def reduce_rows(block):
        took(half_in.at[block], red_recv, block, 0)
        half[block] = raw[block, pl.ds(core * J, J)] + half_in[block]

        def one(k, carry):
            to = (j + k) % J
            remote(half.at[block, to], row_in.at[block, j], block, 1, (a, to * C + core)).start()
            return carry

        lax.fori_loop(1, J, one, 0)
        row_in[block, j] = half[block, j]

    def summed(ref, block, count):
        value = ref[block, 0]
        for i in range(1, count):
            value = value + ref[block, i]
        return value

    def reduce_x(block):
        took(row_in.at[block, pl.ds(0, J - 1)], red_recv, block, 1)
        x_in[block, x] = summed(row_in, block, J)

        def one(k, carry):
            remote(x_in.at[block, x], x_in.at[block, x], block, 2, ((x + k) % X * ZH + zh, b)).start()
            return carry

        lax.fori_loop(1, X, one, 0)

    def reduce_z(block):
        took(x_in.at[block, pl.ds(0, X - 1)], red_recv, block, 2)
        z_in[block, zh] = summed(x_in, block, X)

        def one(k, carry):
            remote(z_in.at[block, zh], z_in.at[block, zh], block, 3, (x * ZH + (zh + k) % ZH, b)).start()
            return carry

        lax.fori_loop(1, ZH, one, 0)

    def gather_rows(block):
        took(z_in.at[block, pl.ds(0, ZH - 1)], red_recv, block, 3)
        slot = core * J + j
        total[block, slot] = summed(z_in, block, ZH)

        def one(k, carry):
            to = (j + k) % J
            remote(total.at[block, slot], total.at[block, slot], block, 4, (a, to * C + core)).start()
            return carry

        lax.fori_loop(1, J, one, 0)

    def gather_core(block):
        took(total.at[block, pl.ds(0, J - 1)], red_recv, block, 4)
        part = total.at[block, pl.ds(core * J, J)]
        remote(part, part, block, 5, partner).start()

    def gather_done(block):
        took(half_in.at[block], red_recv, block, 5)

    grads[...] = jnp.zeros_like(grads)
    loads[0].wait()
    products(1)
    loads[1].wait()
    loads[2].wait()
    transform(1, 0, load_first, send_b)
    pl.semaphore_wait(barrier, NA + NB - 2)
    send_swap(0, 0)

    def first(c, carry):
        transform(1, c, load_first, send_b)
        send_swap(c, 0)
        return carry

    lax.fori_loop(1, NC, first, 0)
    metrics(1)

    def first_derive(c, carry):
        derive(1, c, load_first)
        return carry

    lax.fori_loop(0, NC, first_derive, 0)
    finish(1)
    reduce_core(1)
    products(0)
    metrics(0)
    reduce_rows(1)

    def second(c, carry):
        wait_swap(c, 0, False)
        transform(0, c, load_second, send_a)
        send_swap(c, 1)
        derive(0, c, load_second)
        return carry

    lax.fori_loop(0, NC, second, 0)
    finish(0)
    reduce_core(0)
    reduce_x(1)
    reduce_rows(0)
    reduce_z(1)
    reduce_x(0)
    gather_rows(1)
    reduce_z(0)
    gather_core(1)
    gather_rows(0)
    gather_done(1)
    gather_core(0)
    gather_done(0)

    def ending(c, carry):
        wait_swap(c, 1, False)
        wait_swap(c, 0, True)
        wait_swap(c, 1, True)
        return carry

    lax.fori_loop(0, NC, ending, 0)
    for block in range(2):
        took(half_in.at[block], red_send, block, 0)
        took(row_in.at[block, pl.ds(0, J - 1)], red_send, block, 1)
        took(x_in.at[block, pl.ds(0, X - 1)], red_send, block, 2)
        took(z_in.at[block, pl.ds(0, ZH - 1)], red_send, block, 3)
        took(total.at[block, pl.ds(0, J - 1)], red_send, block, 4)
        took(half_in.at[block], red_send, block, 5)


def layout_kernel(cfg, fin, total, out_state, out_costate, out_grads):
    NA, NB, ZH, C, SC, G, S, scale = cfg
    for arr, out in ((0, out_state), (1, out_costate)):
        for c in range(S // SC):
            for s in range(SC):
                out[pl.ds(c * SC + s, G, stride=S), :] = fin[c, arr, pl.ds(s, G, stride=SC), :]
    out_grads[...] = total[...]


def shards(zh, cores, state, costate, gates, targets):
    NA, NB = lax.axis_size("qa"), lax.axis_size("qb")
    layout = state.shape
    G, S, L = layout[2:]
    SC = CHUNK
    NC = S // SC
    X, J = NA // zh, NB // cores
    scale = float(NA * NB * G * S) ** -0.5
    cfg = (NA, NB, zh, cores, SC, G, S, scale)
    per = 4 * G // NB
    vmem = pl.BlockSpec(memory_space=pltpu.VMEM)
    fin, total = pl.pallas_call(
        functools.partial(main_kernel, cfg),
        out_shape=(
            jax.ShapeDtypeStruct((NC, 2, G * SC, L), F32),
            jax.ShapeDtypeStruct((2, NB, per, L), F32),
        ),
        in_specs=[pl.BlockSpec(memory_space=pltpu.SMEM)] + [pl.BlockSpec(memory_space=pltpu.HBM)] * 3,
        out_specs=(vmem, vmem),
        scratch_shapes=[
            pltpu.VMEM((G * S, L), F32),
            pltpu.VMEM((G * S, L), F32),
            pltpu.VMEM((8, G, G), F32),
            pltpu.SemaphoreType.DMA((3,)),
            pltpu.VMEM((NC, 2, G * SC, L), F32),
            pltpu.VMEM((NC, 2, G * SC, L), F32),
            pltpu.VMEM((NC, 2, G * SC, L), F32),
            pltpu.VMEM((2, 2 * G, 2 * G), BF16),
            pltpu.VMEM((2, G, 2 * G), BF16),
            pltpu.VMEM((2, 4, G, 2 * G), BF16),
            pltpu.VMEM((2, 4, G, 2 * G), BF16),
            pltpu.VMEM((2, 4, 2 * G, G), BF16),
            pltpu.VMEM((2, 4, G, G), BF16),
            pltpu.VMEM((2, 4, G, G), F32),
            pltpu.VMEM((2, 2 * G, SC * G), BF16),
            pltpu.VMEM((2, G, SC * G), BF16),
            pltpu.VMEM((2, 2 * G, SC * G), BF16),
            pltpu.VMEM((2, 4, G, G), F32),
            pltpu.VMEM((2, NB, per, L), F32),
            pltpu.VMEM((2, J, per, L), F32),
            pltpu.VMEM((2, J, per, L), F32),
            pltpu.VMEM((2, J, per, L), F32),
            pltpu.VMEM((2, X, per, L), F32),
            pltpu.VMEM((2, zh, per, L), F32),
            pltpu.SemaphoreType.DMA((2, NC)),
            pltpu.SemaphoreType.DMA((2, NC)),
            pltpu.SemaphoreType.DMA((2, NC)),
            pltpu.SemaphoreType.DMA((2, 6)),
            pltpu.SemaphoreType.DMA((2, 6)),
        ],
        compiler_params=pltpu.CompilerParams(
            collective_id=0, has_side_effects=True
        ),
        name="adjoint_main",
    )(targets, state.reshape(G * S, L), costate.reshape(G * S, L), gates.reshape(8, G, G))
    out_state, out_costate, grads = pl.pallas_call(
        functools.partial(layout_kernel, cfg),
        out_shape=(
            jax.ShapeDtypeStruct((G * S, L), F32),
            jax.ShapeDtypeStruct((G * S, L), F32),
            jax.ShapeDtypeStruct((2, NB, per, L), F32),
        ),
        in_specs=[vmem, vmem],
        out_specs=(vmem, vmem, vmem),
        name="adjoint_layout",
    )(fin, total)
    return out_state.reshape(layout), out_costate.reshape(layout), grads.reshape(2, 4, G, G)


def build(mesh, zh, cores):
    in_specs = (P("qa", "qb", None, None, None), P("qa", "qb", None, None, None), P(), P())
    out_specs = (P("qa", "qb", None, None, None), P("qa", "qb", None, None, None), P())
    return jax.shard_map(
        functools.partial(shards, zh, cores), mesh=mesh, in_specs=in_specs, out_specs=out_specs, check_vma=False
    )


def solution(mesh):
    return build(mesh, Z_HI, CORES)
```
